128 devices in a mesh: row: 8 (over z, x_hi), col: 16 (over x_lo, y, core).
Axes of the slice: x: 4 (x_hi: 2, x_lo: 2; x = x_hi * 2 + x_lo), y: 4, z: 4, core: 2. Of those that a mesh axis runs over, the one named last changes fastest.
Arguments:
- ingest_features: bfloat16 [32768, 1536], P(('row', 'col')), may hold values from -40 to 40
- node_map: int32 [32768], P(('row', 'col')), may hold values from 0 to 16383, as said below
- unit_rows: int32 [128], P(('row', 'col')), may hold values from 0 to 256, as said below
- tile_ids: int32 [12288, 2], P(('row', 'col')), may hold values from 0 to 128, as said below
- tile_values: bfloat16 [12288, 128, 128], P(('row', 'col')), may hold values from -40 to 40
- mix_in: bfloat16 [128, 128], replicated, may hold values from -0.5 to 0.5
- mix_out: bfloat16 [128, 128], replicated, may hold values from -0.5 to 0.5
Outputs:
- residual: float32 [16384, 1536], P(('row', 'col'))
The draws below stay inside these ranges and needn't reach their ends.
Inputs may be any that keep to these rules, and one draw needn't show every extreme that they name: `node_map`: for every unit u the first unit_rows[u] of its 256 slots name distinct nodes, and all units' such slots together name every node exactly once; at most 2 of them of one unit name nodes of one partition (nodes k * 128 to (k + 1) * 128 - 1), and one unit names exactly 2 in every partition. Entries of the other slots are arbitrary nodes. `unit_rows`: one unit delivers 256 rows. `tile_ids`: slots k * 96 to (k + 1) * 96 - 1 hold first some distinct tiles whose row tile lies in row block k // 16 (tile rows (16 times that) onward) and whose column tile lies in column block k % 16, then padding slots whose row tile and column tile are both 16384 // 128. Some blocks have no padding slot.
All inputs are finite; a program needn't handle non-finite values.
Results may differ from the reference program's by a relative error of at most 0.0095.
Values may be sent and summed in bfloat16 or wider, within the bound.
A program may use at most 64 MiB of HBM per device.

```python
import jax
import jax.numpy as jnp
from jax import lax

CH = 128
TILE = 128
PIECE = 128
FEAT = 1536
ROW_GROUPS = 8
COL_GROUPS = 16
INGEST_PARTS = 128
NODES = 16384
ROW_TILES = 16
COL_TILES = 8
TILES_DEV = 96
SLOTS = 12288
PAIR = 2
CAP = 256
N_ROW = 8
N_COL = 16


def ingest_tables(key):
    selection_key, extra_random_key, weighty_random_key, ordering_random_key, padding_random_key = jax.random.split(key, 5)
    total_slot_count = INGEST_PARTS * PAIR
    owning_partition = jnp.arange(total_slot_count, dtype=jnp.int32) // PAIR
    extra_amount = jax.random.randint(extra_random_key, (INGEST_PARTS,), 0, 256)
    heavy = jax.random.randint(weighty_random_key, (), 0, INGEST_PARTS)
    base_amount = jax.random.randint(selection_key, (INGEST_PARTS, total_slot_count), 0, 1024) + 4 * extra_amount[owning_partition][None, :]
    base_amount = jnp.where((owning_partition == heavy)[None, :], -4096, base_amount)
    score = base_amount * total_slot_count + jnp.arange(total_slot_count, dtype=jnp.int32)[None, :]
    unused, chosen = lax.top_k(-score, PIECE)
    partition = jnp.arange(INGEST_PARTS, dtype=jnp.int32)[:, None]
    placed = partition * PIECE + jnp.arange(PIECE, dtype=jnp.int32)[None, :]
    node_at = jnp.full((INGEST_PARTS, total_slot_count), -1, jnp.int32).at[partition, chosen].set(placed)
    candidates = node_at.reshape(INGEST_PARTS, INGEST_PARTS, PAIR).transpose(1, 0, 2).reshape(INGEST_PARTS, CAP)
    alive = (candidates >= 0).astype(jnp.int32)
    shuffle = jax.random.randint(ordering_random_key, (INGEST_PARTS, CAP), 0, 4096)
    order_score = (1 - alive) * (1 << 25) + shuffle * CAP + jnp.arange(CAP, dtype=jnp.int32)[None, :]
    order = jnp.argsort(order_score, axis=1, stable=True)
    arranged = jnp.take_along_axis(candidates, order, axis=1)
    counts = jnp.sum(alive, axis=1).astype(jnp.int32)
    filler = jax.random.randint(padding_random_key, (INGEST_PARTS, CAP), 0, NODES)
    mapping = jnp.where(arranged >= 0, arranged, filler).reshape(-1).astype(jnp.int32)
    return (mapping, counts)


def draw_node_map(key, part):
    return ingest_tables(jax.random.fold_in(key, 5))[0]


def draw_unit_rows(key, part):
    return ingest_tables(jax.random.fold_in(key, 5))[1]


def tile_layout(key):

    def one_device(device):
        row_block = device // COL_GROUPS
        col_block = device % COL_GROUPS
        near = (col_block * N_ROW < (row_block + 1) * N_COL) & (row_block * N_COL < (col_block + 1) * N_ROW)
        few = jax.random.randint(jax.random.fold_in(key, device + 7919), (), TILES_DEV // 8, TILES_DEV // 4 + 1)
        count = jnp.where(near, TILES_DEV, few)
        order = jax.random.permutation(jax.random.fold_in(key, device), ROW_TILES * COL_TILES)[:TILES_DEV]
        row_tile = order // COL_TILES + row_block * ROW_TILES
        col_tile = order % COL_TILES + col_block * COL_TILES
        real = jnp.arange(TILES_DEV, dtype=jnp.int32) < count
        pad = NODES // TILE
        row_tile = jnp.where(real, row_tile, pad)
        col_tile = jnp.where(real, col_tile, pad)
        return jnp.stack([row_tile, col_tile], axis=-1).astype(jnp.int32)
    return jax.vmap(one_device)(jnp.arange(INGEST_PARTS, dtype=jnp.int32)).reshape(SLOTS, 2)


def draw_tile_ids(key, part):
    return tile_layout(jax.random.fold_in(key, 11))


def draw_tile_values(key, part):
    layout = jnp.minimum(tile_layout(jax.random.fold_in(key, 11)), NODES // TILE - 1)
    row_key, col_key, entry_key = jax.random.split(jax.random.fold_in(key, 12), 3)
    low = jnp.log(0.3)
    high = jnp.log(3.0)
    row_scale = jnp.exp(jax.random.uniform(row_key, (NODES,), jnp.float32, low, high))
    col_scale = jnp.exp(jax.random.uniform(col_key, (NODES,), jnp.float32, low, high))
    inside = jnp.arange(TILE, dtype=jnp.int32)[None, :]
    row_part = row_scale[layout[:, 0:1] * TILE + inside]
    col_part = col_scale[layout[:, 1:2] * TILE + inside]
    entries = jnp.clip(jax.random.normal(entry_key, (SLOTS, TILE, TILE), jnp.float32), -4.0, 4.0)
    return (entries * row_part[:, :, None] * col_part[:, None, :]).astype(jnp.bfloat16)


def draw_ingest_features(key, part):
    slot_key, column_key, entry_key = jax.random.split(key, 3)
    low = jnp.log(0.3)
    high = jnp.log(3.0)
    slot_scale = jnp.exp(jax.random.uniform(slot_key, (INGEST_PARTS * CAP, 1), jnp.float32, low, high))
    column_scale = jnp.exp(jax.random.uniform(column_key, (1, FEAT), jnp.float32, low, high))
    entries = jnp.clip(jax.random.normal(entry_key, (INGEST_PARTS * CAP, FEAT), jnp.float32), -4.0, 4.0)
    return (entries * slot_scale * column_scale).astype(jnp.bfloat16)


def scatter_about(stream_key, dims, scale, reach, kind=jnp.bfloat16):
    values = jax.random.normal(stream_key, dims, jnp.float32) * scale
    return jnp.minimum(jnp.maximum(values, -reach), reach).astype(kind)


def setup_inputs(seed: int = 0) -> dict:
    key_list = jax.random.split(jax.random.key(seed), 8)
    return {
        "ingest_features": draw_ingest_features(jax.random.fold_in(key_list[7], 71), 0),
        "node_map": draw_node_map(jax.random.fold_in(key_list[7], 71), 0),
        "unit_rows": draw_unit_rows(jax.random.fold_in(key_list[7], 71), 0),
        "tile_ids": draw_tile_ids(jax.random.fold_in(key_list[7], 71), 0),
        "tile_values": draw_tile_values(jax.random.fold_in(key_list[7], 71), 0),
        "mix_in": scatter_about(key_list[5], (CH, CH), CH ** -0.5, 0.5),
        "mix_out": scatter_about(key_list[6], (CH, CH), CH ** -0.5, 0.5),
    }


epsilon = 1e-05

def normalize(values):
    groups = values.reshape(-1, CH)
    power = lax.optimization_barrier(jnp.mean(groups * groups, axis=-1, keepdims=True))
    return (groups * lax.rsqrt(power + epsilon)).astype(jnp.bfloat16)

def encode(totals, mix_in):
    row_total = totals.shape[0]
    mixed = jnp.dot(normalize(totals), mix_in, preferred_element_type=jnp.float32)
    return jax.nn.gelu(mixed, approximate=False).astype(jnp.bfloat16).reshape(row_total, -1)

def dense_block(tile_ids, tile_values, row_index, col_index, row_tiles, col_tiles):
    local_rows = tile_ids[:, 0] - row_index * row_tiles
    local_cols = tile_ids[:, 1] - col_index * col_tiles
    tile_edge = tile_values.shape[1]
    tile_grid = jnp.zeros((row_tiles, col_tiles, tile_edge, tile_edge), tile_values.dtype)
    tile_grid = tile_grid.at[local_rows, local_cols].set(tile_values, mode='drop')
    return tile_grid.transpose(0, 2, 1, 3).reshape(row_tiles * tile_edge, col_tiles * tile_edge)

def reference(ingest_features, node_map, unit_rows, tile_ids, tile_values, mix_in, mix_out):
    live = (jnp.arange(CAP, dtype=jnp.int32)[None, :] < unit_rows[:, None]).reshape(-1)
    target = jnp.where(live, node_map, NODES)
    features = jnp.zeros((NODES, FEAT), jnp.bfloat16).at[target].set(ingest_features, mode='drop')
    span_rows = ROW_TILES * TILE
    span_cols = COL_TILES * TILE

    def block_at(row_index, col_index):
        device = row_index * COL_GROUPS + col_index
        chosen_ids = lax.dynamic_slice_in_dim(tile_ids, device * TILES_DEV, TILES_DEV, 0)
        chosen_values = lax.dynamic_slice_in_dim(tile_values, device * TILES_DEV, TILES_DEV, 0)
        return dense_block(chosen_ids, chosen_values, row_index, col_index, ROW_TILES, COL_TILES)

    def back_parts(row_index, panel):

        def one_part(col_index):
            product = lax.dot_general(block_at(row_index, col_index), panel, (((0,), (0,)), ((), ())), preferred_element_type=jnp.float32)
            return product.astype(jnp.bfloat16)
        return lax.map(one_part, jnp.arange(COL_GROUPS, dtype=jnp.int32))
    back_sum = jnp.zeros((NODES, FEAT), jnp.float32)
    for row_index in range(ROW_GROUPS):
        panel = features[row_index * span_rows:(row_index + 1) * span_rows]
        back_sum = back_sum + back_parts(row_index, panel).reshape(NODES, FEAT).astype(jnp.float32)
    hidden = encode(back_sum, mix_in)

    def forward_parts(col_index, panel):

        def one_part(row_index):
            product = jnp.dot(block_at(row_index, col_index), panel, preferred_element_type=jnp.float32)
            return product.astype(jnp.bfloat16)
        return lax.map(one_part, jnp.arange(ROW_GROUPS, dtype=jnp.int32))
    forward_sum = jnp.zeros((NODES, FEAT), jnp.float32)
    for col_index in range(COL_GROUPS):
        panel = hidden[col_index * span_cols:(col_index + 1) * span_cols]
        forward_sum = forward_sum + forward_parts(col_index, panel).reshape(NODES, FEAT).astype(jnp.float32)
    recon = jnp.dot(normalize(forward_sum), mix_out, preferred_element_type=jnp.float32).reshape(NODES, FEAT)
    return features.astype(jnp.float32) - recon
```

```python
import functools

import jax
import jax.numpy as jnp
from jax import lax
from jax.experimental import pallas as pl
from jax.experimental.pallas import tpu as pltpu
from jax.sharding import PartitionSpec as P

CH = 128
TILE = 128
PIECE = 128
CHUNKS = 3
LAG = 3
MESH = pl.DeviceIdType.MESH

epsilon = 1e-05


def normalize(groups):
    power = jnp.mean(groups * groups, axis=-1, keepdims=True)
    return (groups * lax.rsqrt(power + epsilon)).astype(jnp.bfloat16)


def gelu(v):
    return 0.5 * v * (1.0 + lax.erf(v * (0.5**0.5)))


class Ring:
    def __init__(self, place, bit, forward, backward, mate):
        self.place, self.bit = place, bit
        self.forward, self.backward, self.mate = forward, backward, mate

    def slot(self, step, other):
        bit = 1 - self.bit if other else self.bit
        return lax.rem(self.place + step + 4, 4) * 2 + bit


def block_kernel(slot_ref, tiles_ref, block_ref, flipped_ref):
    place = pl.program_id(0)
    for col in range(block_ref.shape[1] // TILE):
        slot = slot_ref[place * (block_ref.shape[1] // TILE) + col]
        tile = tiles_ref[jnp.maximum(slot, 0)]
        tile = jnp.where(slot >= 0, tile, jnp.zeros_like(tile))
        block_ref[:, col * TILE : (col + 1) * TILE] = tile
        flipped_ref[col * TILE : (col + 1) * TILE, :] = tile.T


def build_block(slot_of, tile_values, row_tiles, col_tiles):
    rows, cols = row_tiles * TILE, col_tiles * TILE
    return pl.pallas_call(
        block_kernel,
        grid_spec=pltpu.PrefetchScalarGridSpec(
            num_scalar_prefetch=1,
            grid=(row_tiles,),
            in_specs=[pl.BlockSpec(tile_values.shape, lambda i, s: (0, 0, 0))],
            out_specs=[
                pl.BlockSpec((TILE, cols), lambda i, s: (i, 0)),
                pl.BlockSpec((cols, TILE), lambda i, s: (0, i)),
            ],
        ),
        out_shape=[
            jax.ShapeDtypeStruct((rows, cols), jnp.bfloat16),
            jax.ShapeDtypeStruct((cols, rows), jnp.bfloat16),
        ],
        cost_estimate=pl.CostEstimate(flops=0, bytes_accessed=24 << 20, transcendentals=0),
        name="build_block",
    )(slot_of, tile_values)


def hops_kernel(
    features_ref, block_hbm, flipped_hbm, mix_in_ref, mix_out_ref, out_ref,
    block, flipped, panel, back, hidden, ahead, across,
    row_near, row_pair, row_sum, row_mate, col_near, col_pair, col_sum, col_mate,
    local_sem, panel_send, panel_recv, core_send, core_recv, hidden_send, hidden_recv,
    row_send, row_recv, col_send, col_recv, swap_send, swap_recv,
):
    width = panel.shape[-1]
    r, q = lax.axis_index("row"), lax.axis_index("col")
    core, y, xl = lax.rem(q, 2), lax.rem(q // 2, 4), q // 8
    z, xh = r // 2, lax.rem(r, 2)

    def col_of(xl_, y_, core_):
        return {"col": (xl_ * 4 + y_) * 2 + core_}

    def row_of(z_, xh_):
        return {"row": z_ * 2 + xh_}

    partner = col_of(xl, y, 1 - core)
    col_ring = Ring(
        y, xl, col_of(xl, lax.rem(y + 1, 4), core), col_of(xl, lax.rem(y + 3, 4), core), col_of(1 - xl, y, core)
    )
    row_ring = Ring(
        z, xh, row_of(lax.rem(z + 1, 4), xh), row_of(lax.rem(z + 3, 4), xh), row_of(z, 1 - xh)
    )

    block_copy = pltpu.make_async_copy(block_hbm, block, local_sem.at[0])
    flipped_copy = pltpu.make_async_copy(flipped_hbm, flipped, local_sem.at[1])
    flipped_copy.start()
    block_copy.start()

    barrier = pltpu.get_barrier_semaphore()
    neighbours = [partner] + [d for g in (col_ring, row_ring) for d in (g.forward, g.backward, g.mate)]
    for device in neighbours:
        pl.semaphore_signal(barrier, inc=1, device_id=device, device_id_type=MESH)
    pl.semaphore_wait(barrier, len(neighbours))

    sent = []

    def send(src, dst, send_sem, recv_sem, device):
        copy = pltpu.make_async_remote_copy(
            src_ref=src, dst_ref=dst, send_sem=send_sem, recv_sem=recv_sem, device_id=device, device_id_type=MESH
        )
        copy.start()
        sent.append(copy)

    def await_recv(dst, send_sem, recv_sem, device):
        pltpu.make_async_remote_copy(
            src_ref=dst, dst_ref=dst, send_sem=send_sem, recv_sem=recv_sem, device_id=device, device_id_type=MESH
        ).wait_recv()

    class Gather:
        def __init__(self, c, ring, buf, base, send_sem, recv_sem):
            self.c, self.ring, self.buf, self.base = c, ring, buf, base
            self.ss, self.rs = send_sem, recv_sem
            self.slots = [
                ring.slot(0, True), ring.slot(-1, False), ring.slot(1, False), ring.slot(-1, True),
                ring.slot(1, True), ring.slot(2, False), ring.slot(2, True),
            ]

        def at(self, slot):
            return self.buf.at[self.c, self.base + slot]

        def push(self, src, slot, kind, device):
            send(src, self.at(slot), self.ss.at[self.c, kind], self.rs.at[self.c, kind], device)

        def wait(self, kind):
            await_recv(self.at(self.slots[kind]), self.ss.at[self.c, kind], self.rs.at[self.c, kind], self.ring.mate)

        def first(self, src):
            own = self.ring.slot(0, False)
            self.push(src, own, 0, self.ring.mate)
            self.push(src, own, 1, self.ring.forward)
            self.push(src, own, 2, self.ring.backward)

        def second(self):
            self.wait(0)
            slot = self.slots[0]
            self.push(self.at(slot), slot, 3, self.ring.forward)
            self.push(self.at(slot), slot, 4, self.ring.backward)

        def third(self, also=None):
            self.wait(1)
            self.push(self.at(self.slots[1]), self.slots[1], 5, self.ring.forward)
            self.wait(2)
            self.wait(4)
            self.push(self.at(self.slots[4]), self.slots[4], 6, self.ring.backward)
            self.wait(3)

        def fourth(self):
            self.wait(5)
            self.wait(6)

    class Scatter:
        def __init__(self, c, ring, buf, base, near, pair, total, mate, send_sem, recv_sem):
            self.c, self.ring, self.buf, self.base = c, ring, buf, base
            self.near, self.pair, self.total, self.mate = near, pair, total, mate
            self.ss, self.rs = send_sem, recv_sem

        def at(self, slot):
            return self.buf.at[self.c, self.base + slot]

        def group(self, step):
            return self.buf.at[self.c, pl.ds(self.base + lax.rem(self.ring.place + step + 4, 4) * 2, 2)]

        def push(self, src, dst, kind, device):
            send(src, dst, self.ss.at[self.c, kind], self.rs.at[self.c, kind], device)

        def wait(self, dst, kind):
            await_recv(dst, self.ss.at[self.c, kind], self.rs.at[self.c, kind], self.ring.mate)

        def first(self):
            self.push(self.at(self.ring.slot(2, False)), self.near.at[self.c, 0], 0, self.ring.forward)
            self.push(self.at(self.ring.slot(2, True)), self.near.at[self.c, 1], 1, self.ring.backward)

        def second(self):
            for kind, step, other, device in ((0, 1, False, self.ring.forward), (1, -1, True, self.ring.backward)):
                self.wait(self.near.at[self.c, kind], kind)
                slot = self.base + self.ring.slot(step, other)
                self.buf[self.c, slot] = (
                    self.buf[self.c, slot].astype(jnp.float32) + self.near[self.c, kind].astype(jnp.float32)
                ).astype(jnp.bfloat16)
                self.push(self.group(step), self.pair.at[self.c, kind], 2 + kind, device)

        def three(self, bit):
            slot = self.base + self.ring.place * 2 + bit
            return (
                self.buf[self.c, slot].astype(jnp.float32)
                + self.pair[self.c, 0, bit].astype(jnp.float32)
                + self.pair[self.c, 1, bit].astype(jnp.float32)
            )

        def third(self):
            self.wait(self.pair.at[self.c, 0], 2)
            self.wait(self.pair.at[self.c, 1], 3)
            self.total[self.c] = self.three(1 - self.ring.bit).astype(jnp.bfloat16)
            self.push(self.total.at[self.c], self.mate.at[self.c], 4, self.ring.mate)

        def last(self):
            self.wait(self.mate.at[self.c], 4)
            return self.three(self.ring.bit) + self.mate[self.c].astype(jnp.float32)

    class Chunk:
        def __init__(self, c):
            self.c = c
            self.cols = slice(c * width, (c + 1) * width)
            self.mine = core * 8
            self.spread = Gather(c, col_ring, panel, self.mine, panel_send, panel_recv)
            self.back = Scatter(
                c, row_ring, back, 0, row_near, row_pair, row_sum, row_mate, row_send, row_recv
            )
            self.share = Gather(c, row_ring, hidden, 0, hidden_send, hidden_recv)
            self.ahead = Scatter(
                c, col_ring, ahead, self.mine, col_near, col_pair, col_sum, col_mate, col_send, col_recv
            )

        def to_partner(self, src, slot, kind):
            send(
                src, panel.at[self.c, self.mine + slot],
                core_send.at[self.c, kind], core_recv.at[self.c, kind], partner,
            )

        def pass_on(self, kinds):
            for kind in kinds:
                slot = self.spread.slots[kind]
                self.to_partner(self.spread.at(slot), slot, kind)

        def s0(self):
            own = features_ref.at[:, self.cols]
            self.spread.first(own)
            self.to_partner(own, col_ring.slot(0, False), 7)
            panel[self.c, self.mine + col_ring.slot(0, False)] = features_ref[:, self.cols]

        def s1(self):
            self.spread.second()
            self.pass_on([0])

        def s2(self):
            self.spread.third()
            self.pass_on([1, 2, 3, 4])

        def s3(self):
            self.spread.fourth()
            self.pass_on([5, 6])

        def s4(self):
            theirs = (1 - core) * 8
            slots = self.spread.slots + [col_ring.slot(0, False)]
            for kind in range(8):
                await_recv(
                    panel.at[self.c, theirs + slots[kind]],
                    core_send.at[self.c, kind], core_recv.at[self.c, kind], partner,
                )
            if self.c == 0:
                flipped_copy.wait()

            @pl.loop(0, 2)
            def _(i):
                lhs = flipped[pl.ds(pl.multiple_of(i * 512, 512), 512), :]
                part = jnp.dot(
                    lhs, panel[self.c].reshape(16 * PIECE, width), preferred_element_type=jnp.float32
                )
                back[self.c, pl.ds(i * 4, 4)] = part.astype(jnp.bfloat16).reshape(4, PIECE, width)

            self.back.first()

        def s5(self):
            self.back.second()

        def s6(self):
            self.back.third()

        def s7(self):
            sums = self.back.last()
            own = row_ring.slot(0, False)
            for k in range(width // CH):
                mixed = jnp.dot(
                    normalize(sums[:, k * CH : (k + 1) * CH]), mix_in_ref[...], preferred_element_type=jnp.float32
                )
                hidden[self.c, own, :, k * CH : (k + 1) * CH] = gelu(mixed).astype(jnp.bfloat16)
            self.share.first(self.share.at(own))

        def s8(self):
            self.share.second()

        def s9(self):
            self.share.third()

        def s10(self):
            self.share.fourth()
            if self.c == 0:
                block_copy.wait()

            @pl.loop(0, 4)
            def _(i):
                half = lax.rem(i // 2 + 1 - core + 2, 2)
                place = half * 2 + lax.rem(i, 2)
                lhs = block[pl.ds(pl.multiple_of(place * 512, 512), 512), :]
                part = jnp.dot(
                    lhs, hidden[self.c].reshape(8 * PIECE, width), preferred_element_type=jnp.float32
                )
                ahead[self.c, pl.ds(place * 4, 4)] = part.astype(jnp.bfloat16).reshape(4, PIECE, width)

            send(
                ahead.at[self.c, pl.ds((1 - core) * 8, 8)], across.at[self.c],
                swap_send.at[self.c], swap_recv.at[self.c], partner,
            )

        def s11(self):
            await_recv(across.at[self.c], swap_send.at[self.c], swap_recv.at[self.c], partner)

            @pl.loop(0, 8)
            def _(i):
                ahead[self.c, self.mine + i] = (
                    ahead[self.c, self.mine + i].astype(jnp.float32) + across[self.c, i].astype(jnp.float32)
                ).astype(jnp.bfloat16)

            self.ahead.first()

        def s12(self):
            self.ahead.second()

        def s13(self):
            self.ahead.third()

        def s14(self):
            sums = self.ahead.last()
            for k in range(width // CH):
                at = slice(self.c * width + k * CH, self.c * width + (k + 1) * CH)
                recon = jnp.dot(
                    normalize(sums[:, k * CH : (k + 1) * CH]), mix_out_ref[...], preferred_element_type=jnp.float32
                )
                out_ref[:, at] = features_ref[:, at].astype(jnp.float32) - recon

    chunks = [Chunk(c) for c in range(CHUNKS)]
    for tick in range(15 + LAG * (CHUNKS - 1)):
        for c in range(CHUNKS):
            stage = tick - LAG * c
            if 0 <= stage < 15:
                getattr(chunks[c], "s%d" % stage)()
    for copy in sent:
        copy.wait_send()


def two_hops(features, block, flipped, mix_in, mix_out):
    feat = features.shape[1]
    width = feat // CHUNKS
    dma = pltpu.SemaphoreType.DMA

    def buf(*shape):
        return pltpu.VMEM((CHUNKS,) + shape + (PIECE, width), jnp.bfloat16)

    vmem = pl.BlockSpec(memory_space=pltpu.VMEM)
    hbm = pl.BlockSpec(memory_space=pl.ANY)
    scatter = [buf(2), buf(2, 2), buf(), buf()]
    return pl.pallas_call(
        hops_kernel,
        out_shape=jax.ShapeDtypeStruct((PIECE, feat), jnp.float32),
        in_specs=[vmem, hbm, hbm, vmem, vmem],
        out_specs=vmem,
        scratch_shapes=[
            pltpu.VMEM(block.shape, jnp.bfloat16),
            pltpu.VMEM(flipped.shape, jnp.bfloat16),
            buf(16), buf(8), buf(8), buf(16), buf(8),
            *scatter, *scatter,
            dma((2,)),
            dma((CHUNKS, 7)), dma((CHUNKS, 7)),
            dma((CHUNKS, 8)), dma((CHUNKS, 8)),
            dma((CHUNKS, 7)), dma((CHUNKS, 7)),
            dma((CHUNKS, 5)), dma((CHUNKS, 5)),
            dma((CHUNKS, 5)), dma((CHUNKS, 5)),
            dma((CHUNKS,)), dma((CHUNKS,)),
        ],
        compiler_params=pltpu.CompilerParams(
            collective_id=0, has_side_effects=True, vmem_limit_bytes=60 << 20
        ),
        name="two_hops",
    )(features, block, flipped, mix_in, mix_out)


def local(ingest_features, node_map, unit_rows, tile_ids, tile_values, mix_in, mix_out):
    row_count = lax.axis_size("row")
    col_count = lax.axis_size("col")
    unit_count = row_count * col_count
    slots_held = node_map.shape[0]
    per_pair = slots_held // unit_count
    feature_width = ingest_features.shape[1]
    row_tiles = col_count * PIECE // TILE
    col_tiles = row_count * PIECE // TILE

    local_rows = tile_ids[:, 0] - lax.axis_index("row") * row_tiles
    local_cols = tile_ids[:, 1] - lax.axis_index("col") * col_tiles
    place = (lax.rem(local_rows, 2) * 4 + lax.rem(local_rows // 2, 4)) * 2 + local_rows // 8
    real = tile_ids[:, 0] < unit_count * PIECE // TILE
    spot = jnp.where(real, place * col_tiles + local_cols, -1)
    slot_ids = jnp.arange(tile_ids.shape[0], dtype=jnp.int32)
    slot_of = jnp.max(
        jnp.where(
            spot[None, :] == jnp.arange(row_tiles * col_tiles, dtype=jnp.int32)[:, None], slot_ids[None, :], -1
        ),
        axis=1,
    )
    block, flipped = build_block(slot_of, tile_values, row_tiles, col_tiles)

    owner = node_map // PIECE
    slot = jnp.arange(slots_held, dtype=jnp.int32)
    live = slot < unit_rows[0]
    same = (owner[:, None] == owner[None, :]) & live[None, :] & (slot[None, :] < slot[:, None])
    rank_within = jnp.sum(same.astype(jnp.int32), axis=1)
    target = jnp.where(live, owner * per_pair + rank_within, -1)
    pick = (target[None, :] == slot[:, None]).astype(jnp.bfloat16)
    marks = jnp.broadcast_to((node_map % PIECE + 1).astype(jnp.bfloat16)[:, None], (slots_held, CH))
    outgoing = jnp.dot(
        pick, jnp.concatenate([ingest_features, marks], axis=1), preferred_element_type=jnp.float32
    ).astype(jnp.bfloat16)
    arrived = lax.all_to_all(
        outgoing.reshape(unit_count, per_pair, feature_width + CH),
        ("row", "col"),
        split_axis=0,
        concat_axis=0,
        tiled=True,
    ).reshape(-1, feature_width + CH)
    arrived_at = arrived[:, feature_width].astype(jnp.int32) - 1
    put = (arrived_at[None, :] == jnp.arange(PIECE, dtype=jnp.int32)[:, None]).astype(jnp.bfloat16)
    features = jnp.dot(put, arrived[:, :feature_width], preferred_element_type=jnp.float32).astype(jnp.bfloat16)
    return two_hops(features, block, flipped, mix_in, mix_out)


def solution(mesh):
    return jax.shard_map(
        local,
        mesh=mesh,
        in_specs=(
            P(("row", "col"), None),
            P(("row", "col")),
            P(("row", "col")),
            P(("row", "col"), None),
            P(("row", "col"), None, None),
            P(),
            P(),
        ),
        out_specs=P(("row", "col"), None),
        check_vma=False,
    )
```

```python
import functools

import jax
import jax.numpy as jnp
from jax import lax
from jax.experimental import pallas as pl
from jax.experimental.pallas import tpu as pltpu
from jax.sharding import PartitionSpec as P

CH = 128
TILE = 128
PIECE = 128
CHUNKS = 6
ORDER = (
    (0, 0), (1, 0), (2, 0), (0, 3), (0, 2), (0, 1), (1, 3), (1, 2), (1, 1), (2, 3), (2, 2), (2, 1), (0, 6), (0, 5),
    (0, 4), (1, 5), (1, 6), (2, 5), (0, 7), (1, 4), (3, 0), (0, 8), (1, 7), (2, 7), (2, 6), (2, 4), (4, 0), (1, 8),
    (3, 3), (3, 2), (3, 1), (0, 10), (0, 9), (4, 3), (4, 2), (4, 1), (2, 8), (5, 0), (1, 10), (1, 9), (3, 6),
    (3, 5), (3, 4), (4, 5), (0, 11), (4, 6), (5, 3), (5, 1), (2, 10), (2, 9), (3, 7), (4, 4), (5, 2), (3, 8),
    (1, 11), (4, 7), (5, 5), (5, 4), (0, 12), (5, 6), (4, 8), (2, 11), (5, 7), (3, 10), (3, 9), (5, 8), (0, 15),
    (0, 14), (1, 12), (4, 10), (4, 9), (0, 13), (3, 11), (5, 10), (5, 9), (2, 12), (0, 18), (1, 15), (1, 14),
    (1, 13), (0, 17), (4, 11), (3, 12), (0, 16), (2, 13), (2, 15), (5, 11), (1, 17), (2, 14), (4, 12), (0, 19),
    (1, 18), (0, 20), (1, 16), (3, 15), (3, 13), (2, 17), (3, 14), (1, 19), (2, 16), (1, 20), (0, 21), (2, 18),
    (4, 15), (5, 12), (3, 17), (4, 14), (4, 13), (2, 19), (3, 16), (2, 20), (0, 23), (0, 22), (1, 21), (3, 18),
    (5, 15), (5, 14), (3, 19), (3, 20), (2, 21), (4, 18), (4, 17), (4, 16), (5, 13), (0, 24), (5, 18), (1, 23),
    (1, 22), (3, 21), (2, 23), (2, 22), (4, 19), (5, 16), (4, 20), (0, 25), (5, 17), (1, 24), (3, 23), (3, 22),
    (4, 21), (5, 19), (5, 20), (1, 25), (2, 24), (3, 24), (5, 21), (4, 23), (2, 25), (4, 22), (3, 25), (5, 23),
    (5, 22), (4, 24), (5, 24), (4, 25), (5, 25),
)
MESH = pl.DeviceIdType.MESH

epsilon = 1e-05


def normalize(groups):
    power = jnp.mean(groups * groups, axis=-1, keepdims=True)
    return (groups * lax.rsqrt(power + epsilon)).astype(jnp.bfloat16)


def gelu(v):
    return 0.5 * v * (1.0 + lax.erf(v * (0.5**0.5)))


class Ring:
    def __init__(self, place, bit, forward, backward, mate):
        self.place, self.bit = place, bit
        self.forward, self.backward, self.mate = forward, backward, mate

    def slot(self, step, other):
        bit = 1 - self.bit if other else self.bit
        return lax.rem(self.place + step + 4, 4) * 2 + bit


def block_kernel(slot_ref, tiles_ref, block_ref, flipped_ref):
    place = pl.program_id(0)
    for col in range(block_ref.shape[1] // TILE):
        slot = slot_ref[place * (block_ref.shape[1] // TILE) + col]
        tile = tiles_ref[jnp.maximum(slot, 0)]
        tile = jnp.where(slot >= 0, tile, jnp.zeros_like(tile))
        block_ref[:, col * TILE : (col + 1) * TILE] = tile
        flipped_ref[col * TILE : (col + 1) * TILE, :] = tile.T


def build_block(slot_of, tile_values, row_tiles, col_tiles):
    rows, cols = row_tiles * TILE, col_tiles * TILE
    return pl.pallas_call(
        block_kernel,
        grid_spec=pltpu.PrefetchScalarGridSpec(
            num_scalar_prefetch=1,
            grid=(row_tiles,),
            in_specs=[pl.BlockSpec(tile_values.shape, lambda i, s: (0, 0, 0))],
            out_specs=[
                pl.BlockSpec((TILE, cols), lambda i, s: (i, 0)),
                pl.BlockSpec((cols, TILE), lambda i, s: (0, i)),
            ],
        ),
        out_shape=[
            jax.ShapeDtypeStruct((rows, cols), jnp.bfloat16),
            jax.ShapeDtypeStruct((cols, rows), jnp.bfloat16),
        ],
        cost_estimate=pl.CostEstimate(flops=0, bytes_accessed=24 << 20, transcendentals=0),
        name="build_block",
    )(slot_of, tile_values)


def hops_kernel(
    features_ref, block_hbm, flipped_hbm, mix_in_ref, mix_out_ref, out_ref,
    block, flipped, panel, back, hidden, ahead, across,
    row_near, row_pair, row_sum, row_mate, col_near, col_pair, col_sum, col_mate,
    local_sem, panel_send, panel_recv, core_send, core_recv, hidden_send, hidden_recv,
    row_send, row_recv, col_send, col_recv, swap_send, swap_recv,
):
    width = panel.shape[-1]
    r, q = lax.axis_index("row"), lax.axis_index("col")
    core, y, xl = lax.rem(q, 2), lax.rem(q // 2, 4), q // 8
    z, xh = r // 2, lax.rem(r, 2)

    def col_of(xl_, y_, core_):
        return {"col": (xl_ * 4 + y_) * 2 + core_}

    def row_of(z_, xh_):
        return {"row": z_ * 2 + xh_}

    partner = col_of(xl, y, 1 - core)
    col_ring = Ring(
        y, xl, col_of(xl, lax.rem(y + 1, 4), core), col_of(xl, lax.rem(y + 3, 4), core), col_of(1 - xl, y, core)
    )
    row_ring = Ring(
        z, xh, row_of(lax.rem(z + 1, 4), xh), row_of(lax.rem(z + 3, 4), xh), row_of(z, 1 - xh)
    )

    block_copy = pltpu.make_async_copy(block_hbm, block, local_sem.at[0])
    flipped_copy = pltpu.make_async_copy(flipped_hbm, flipped, local_sem.at[1])
    flipped_copy.start()
    block_copy.start()

    barrier = pltpu.get_barrier_semaphore()
    neighbours = [partner] + [d for g in (col_ring, row_ring) for d in (g.forward, g.backward, g.mate)]
    for device in neighbours:
        pl.semaphore_signal(barrier, inc=1, device_id=device, device_id_type=MESH)
    pl.semaphore_wait(barrier, len(neighbours))

    sent = []

    def send(src, dst, send_sem, recv_sem, device):
        copy = pltpu.make_async_remote_copy(
            src_ref=src, dst_ref=dst, send_sem=send_sem, recv_sem=recv_sem, device_id=device, device_id_type=MESH
        )
        copy.start()
        sent.append(copy)

    def await_recv(dst, send_sem, recv_sem, device):
        pltpu.make_async_remote_copy(
            src_ref=dst, dst_ref=dst, send_sem=send_sem, recv_sem=recv_sem, device_id=device, device_id_type=MESH
        ).wait_recv()

    class Gather:
        def __init__(self, c, ring, buf, base, send_sem, recv_sem):
            self.c, self.ring, self.buf, self.base = c, ring, buf, base
            self.ss, self.rs = send_sem, recv_sem
            self.slots = [
                ring.slot(0, True), ring.slot(-1, False), ring.slot(1, False), ring.slot(-1, True),
                ring.slot(1, True), ring.slot(2, False), ring.slot(2, True),
            ]

        def at(self, slot):
            return self.buf.at[self.c, self.base + slot]

        def push(self, src, slot, kind, device):
            send(src, self.at(slot), self.ss.at[self.c, kind], self.rs.at[self.c, kind], device)

        def wait(self, kind):
            await_recv(self.at(self.slots[kind]), self.ss.at[self.c, kind], self.rs.at[self.c, kind], self.ring.mate)

        def first(self, src):
            own = self.ring.slot(0, False)
            self.push(src, own, 0, self.ring.mate)
            self.push(src, own, 1, self.ring.forward)
            self.push(src, own, 2, self.ring.backward)

        def second(self):
            self.wait(0)
            slot = self.slots[0]
            self.push(self.at(slot), slot, 3, self.ring.forward)
            self.push(self.at(slot), slot, 4, self.ring.backward)

        def relay(self, kind):
            self.wait(kind)
            slot = self.slots[kind]
            if kind == 1:
                self.push(self.at(slot), slot, 5, self.ring.forward)
            if kind == 4:
                self.push(self.at(slot), slot, 6, self.ring.backward)

    class Scatter:
        def __init__(self, c, ring, buf, base, near, pair, total, mate, send_sem, recv_sem):
            self.c, self.ring, self.buf, self.base = c, ring, buf, base
            self.near, self.pair, self.total, self.mate = near, pair, total, mate
            self.ss, self.rs = send_sem, recv_sem

        def at(self, slot):
            return self.buf.at[self.c, self.base + slot]

        def group(self, step):
            return self.buf.at[self.c, pl.ds(self.base + lax.rem(self.ring.place + step + 4, 4) * 2, 2)]

        def push(self, src, dst, kind, device):
            send(src, dst, self.ss.at[self.c, kind], self.rs.at[self.c, kind], device)

        def wait(self, dst, kind):
            await_recv(dst, self.ss.at[self.c, kind], self.rs.at[self.c, kind], self.ring.mate)

        def first(self):
            self.push(self.at(self.ring.slot(2, False)), self.near.at[self.c, 0], 0, self.ring.forward)
            self.push(self.at(self.ring.slot(2, True)), self.near.at[self.c, 1], 1, self.ring.backward)

        def second(self, kind):
            step, other, device = ((1, False, self.ring.forward), (-1, True, self.ring.backward))[kind]
            self.wait(self.near.at[self.c, kind], kind)
            slot = self.base + self.ring.slot(step, other)
            self.buf[self.c, slot] = (
                self.buf[self.c, slot].astype(jnp.float32) + self.near[self.c, kind].astype(jnp.float32)
            ).astype(jnp.bfloat16)
            self.push(self.group(step), self.pair.at[self.c, kind], 2 + kind, device)

        def three(self, bit):
            slot = self.base + self.ring.place * 2 + bit
            return (
                self.buf[self.c, slot].astype(jnp.float32)
                + self.pair[self.c, 0, bit].astype(jnp.float32)
                + self.pair[self.c, 1, bit].astype(jnp.float32)
            )

        def third(self):
            self.wait(self.pair.at[self.c, 0], 2)
            self.wait(self.pair.at[self.c, 1], 3)
            self.total[self.c] = self.three(1 - self.ring.bit).astype(jnp.bfloat16)
            self.push(self.total.at[self.c], self.mate.at[self.c], 4, self.ring.mate)

        def last(self):
            self.wait(self.mate.at[self.c], 4)
            return self.three(self.ring.bit) + self.mate[self.c].astype(jnp.float32)

    class Chunk:
        def __init__(self, c):
            self.c = c
            self.cols = slice(c * width, (c + 1) * width)
            self.mine = core * 8
            self.spread = Gather(c, col_ring, panel, self.mine, panel_send, panel_recv)
            self.back = Scatter(
                c, row_ring, back, 0, row_near, row_pair, row_sum, row_mate, row_send, row_recv
            )
            self.share = Gather(c, row_ring, hidden, 0, hidden_send, hidden_recv)
            self.ahead = Scatter(
                c, col_ring, ahead, self.mine, col_near, col_pair, col_sum, col_mate, col_send, col_recv
            )

        def to_partner(self, src, slot, kind):
            send(
                src, panel.at[self.c, self.mine + slot],
                core_send.at[self.c, kind], core_recv.at[self.c, kind], partner,
            )

        def pass_on(self, kind):
            slot = self.spread.slots[kind]
            self.to_partner(self.spread.at(slot), slot, kind)

        def begin(self):
            own = features_ref.at[:, self.cols]
            self.spread.first(own)
            self.to_partner(own, col_ring.slot(0, False), 7)
            panel[self.c, self.mine + col_ring.slot(0, False)] = features_ref[:, self.cols]

        def spread_mate(self):
            self.spread.second()
            self.pass_on(0)

        def spread_relay(self, kind):
            self.spread.relay(kind)
            self.pass_on(kind)

        def back_product(self):
            theirs = (1 - core) * 8
            slots = self.spread.slots + [col_ring.slot(0, False)]
            for kind in range(8):
                await_recv(
                    panel.at[self.c, theirs + slots[kind]],
                    core_send.at[self.c, kind], core_recv.at[self.c, kind], partner,
                )
            if self.c == 0:
                flipped_copy.wait()

            @pl.loop(0, 2)
            def _(i):
                lhs = flipped[pl.ds(pl.multiple_of(i * 512, 512), 512), :]
                part = jnp.dot(
                    lhs, panel[self.c].reshape(16 * PIECE, width), preferred_element_type=jnp.float32
                )
                back[self.c, pl.ds(i * 4, 4)] = part.astype(jnp.bfloat16).reshape(4, PIECE, width)

            self.back.first()

        def encode(self):
            sums = self.back.last()
            own = row_ring.slot(0, False)
            for k in range(width // CH):
                mixed = jnp.dot(
                    normalize(sums[:, k * CH : (k + 1) * CH]), mix_in_ref[...], preferred_element_type=jnp.float32
                )
                hidden[self.c, own, :, k * CH : (k + 1) * CH] = gelu(mixed).astype(jnp.bfloat16)
            self.share.first(self.share.at(own))

        def ahead_product(self):
            if self.c == 0:
                block_copy.wait()

            @pl.loop(0, 4)
            def _(i):
                half = lax.rem(i // 2 + 1 - core + 2, 2)
                place = half * 2 + lax.rem(i, 2)
                lhs = block[pl.ds(pl.multiple_of(place * 512, 512), 512), :]
                part = jnp.dot(
                    lhs, hidden[self.c].reshape(8 * PIECE, width), preferred_element_type=jnp.float32
                )
                ahead[self.c, pl.ds(place * 4, 4)] = part.astype(jnp.bfloat16).reshape(4, PIECE, width)

            send(
                ahead.at[self.c, pl.ds((1 - core) * 8, 8)], across.at[self.c],
                swap_send.at[self.c], swap_recv.at[self.c], partner,
            )

        def join_cores(self):
            await_recv(across.at[self.c], swap_send.at[self.c], swap_recv.at[self.c], partner)

            @pl.loop(0, 8)
            def _(i):
                ahead[self.c, self.mine + i] = (
                    ahead[self.c, self.mine + i].astype(jnp.float32) + across[self.c, i].astype(jnp.float32)
                ).astype(jnp.bfloat16)

            self.ahead.first()

        def decode(self):
            sums = self.ahead.last()
            for k in range(width // CH):
                at = slice(self.c * width + k * CH, self.c * width + (k + 1) * CH)
                recon = jnp.dot(
                    normalize(sums[:, k * CH : (k + 1) * CH]), mix_out_ref[...], preferred_element_type=jnp.float32
                )
                out_ref[:, at] = features_ref[:, at].astype(jnp.float32) - recon

        def steps(self):
            part = functools.partial
            return [
                self.begin,
                self.spread_mate,
                *[part(self.spread_relay, kind) for kind in range(1, 7)],
                self.back_product,
                part(self.back.second, 0),
                part(self.back.second, 1),
                self.back.third,
                self.encode,
                self.share.second,
                *[part(self.share.relay, kind) for kind in range(1, 7)],
                self.ahead_product,
                self.join_cores,
                part(self.ahead.second, 0),
                part(self.ahead.second, 1),
                self.ahead.third,
                self.decode,
            ]

    steps = [Chunk(c).steps() for c in range(CHUNKS)]
    for c, step in ORDER:
        steps[c][step]()
    for copy in sent:
        copy.wait_send()


def two_hops(features, block, flipped, mix_in, mix_out):
    feat = features.shape[1]
    width = feat // CHUNKS
    dma = pltpu.SemaphoreType.DMA

    def buf(*shape):
        return pltpu.VMEM((CHUNKS,) + shape + (PIECE, width), jnp.bfloat16)

    vmem = pl.BlockSpec(memory_space=pltpu.VMEM)
    hbm = pl.BlockSpec(memory_space=pl.ANY)
    scatter = [buf(2), buf(2, 2), buf(), buf()]
    return pl.pallas_call(
        hops_kernel,
        out_shape=jax.ShapeDtypeStruct((PIECE, feat), jnp.float32),
        in_specs=[vmem, hbm, hbm, vmem, vmem],
        out_specs=vmem,
        scratch_shapes=[
            pltpu.VMEM(block.shape, jnp.bfloat16),
            pltpu.VMEM(flipped.shape, jnp.bfloat16),
            buf(16), buf(8), buf(8), buf(16), buf(8),
            *scatter, *scatter,
            dma((2,)),
            dma((CHUNKS, 7)), dma((CHUNKS, 7)),
            dma((CHUNKS, 8)), dma((CHUNKS, 8)),
            dma((CHUNKS, 7)), dma((CHUNKS, 7)),
            dma((CHUNKS, 5)), dma((CHUNKS, 5)),
            dma((CHUNKS, 5)), dma((CHUNKS, 5)),
            dma((CHUNKS,)), dma((CHUNKS,)),
        ],
        compiler_params=pltpu.CompilerParams(
            collective_id=0, has_side_effects=True, vmem_limit_bytes=60 << 20
        ),
        name="two_hops",
    )(features, block, flipped, mix_in, mix_out)


def local(ingest_features, node_map, unit_rows, tile_ids, tile_values, mix_in, mix_out):
    row_count = lax.axis_size("row")
    col_count = lax.axis_size("col")
    unit_count = row_count * col_count
    slots_held = node_map.shape[0]
    per_pair = slots_held // unit_count
    feature_width = ingest_features.shape[1]
    row_tiles = col_count * PIECE // TILE
    col_tiles = row_count * PIECE // TILE

    local_rows = tile_ids[:, 0] - lax.axis_index("row") * row_tiles
    local_cols = tile_ids[:, 1] - lax.axis_index("col") * col_tiles
    place = (lax.rem(local_rows, 2) * 4 + lax.rem(local_rows // 2, 4)) * 2 + local_rows // 8
    real = tile_ids[:, 0] < unit_count * PIECE // TILE
    spot = jnp.where(real, place * col_tiles + local_cols, -1)
    slot_ids = jnp.arange(tile_ids.shape[0], dtype=jnp.int32)
    slot_of = jnp.max(
        jnp.where(
            spot[None, :] == jnp.arange(row_tiles * col_tiles, dtype=jnp.int32)[:, None], slot_ids[None, :], -1
        ),
        axis=1,
    )
    block, flipped = build_block(slot_of, tile_values, row_tiles, col_tiles)

    owner = node_map // PIECE
    slot = jnp.arange(slots_held, dtype=jnp.int32)
    live = slot < unit_rows[0]
    same = (owner[:, None] == owner[None, :]) & live[None, :] & (slot[None, :] < slot[:, None])
    rank_within = jnp.sum(same.astype(jnp.int32), axis=1)
    target = jnp.where(live, owner * per_pair + rank_within, -1)
    pick = (target[None, :] == slot[:, None]).astype(jnp.bfloat16)
    marks = jnp.broadcast_to((node_map % PIECE + 1).astype(jnp.bfloat16)[:, None], (slots_held, CH))
    outgoing = jnp.dot(
        pick, jnp.concatenate([ingest_features, marks], axis=1), preferred_element_type=jnp.float32
    ).astype(jnp.bfloat16)
    arrived = lax.all_to_all(
        outgoing.reshape(unit_count, per_pair, feature_width + CH),
        ("row", "col"),
        split_axis=0,
        concat_axis=0,
        tiled=True,
    ).reshape(-1, feature_width + CH)
    arrived_at = arrived[:, feature_width].astype(jnp.int32) - 1
    put = (arrived_at[None, :] == jnp.arange(PIECE, dtype=jnp.int32)[:, None]).astype(jnp.bfloat16)
    features = jnp.dot(put, arrived[:, :feature_width], preferred_element_type=jnp.float32).astype(jnp.bfloat16)
    return two_hops(features, block, flipped, mix_in, mix_out)


def solution(mesh):
    return jax.shard_map(
        local,
        mesh=mesh,
        in_specs=(
            P(("row", "col"), None),
            P(("row", "col")),
            P(("row", "col")),
            P(("row", "col"), None),
            P(("row", "col"), None, None),
            P(),
            P(),
        ),
        out_specs=P(("row", "col"), None),
        check_vma=False,
    )
```

```python
import functools

import jax
import jax.numpy as jnp
from jax import lax
from jax.experimental import pallas as pl
from jax.experimental.pallas import tpu as pltpu
from jax.sharding import PartitionSpec as P

CH = 128
TILE = 128
PIECE = 128
CHUNKS = 6
ORDER = (
    (0, 0), (1, 0), (0, 1), (0, 2), (0, 3), (1, 1), (1, 2), (1, 3), (2, 0), (0, 5), (0, 4), (0, 6), (1, 5), (2, 1),
    (3, 0), (1, 4), (2, 3), (1, 6), (0, 7), (3, 1), (1, 7), (2, 2), (0, 8), (2, 5), (2, 4), (1, 8), (3, 2), (3, 3),
    (3, 5), (3, 4), (0, 10), (0, 9), (2, 6), (2, 7), (4, 0), (5, 0), (1, 10), (3, 6), (1, 9), (3, 7), (2, 8),
    (4, 1), (3, 8), (5, 1), (0, 11), (4, 2), (5, 2), (4, 3), (5, 3), (4, 5), (4, 4), (1, 11), (2, 10), (2, 9),
    (5, 5), (5, 4), (3, 10), (3, 9), (4, 6), (4, 7), (0, 12), (5, 6), (4, 8), (5, 7), (1, 12), (2, 11), (5, 8),
    (0, 13), (3, 11), (0, 14), (0, 15), (4, 10), (4, 9), (1, 13), (1, 14), (1, 15), (5, 10), (5, 9), (2, 12),
    (0, 17), (0, 16), (0, 18), (3, 12), (1, 17), (4, 11), (2, 13), (1, 16), (1, 18), (3, 13), (2, 15), (5, 11),
    (0, 19), (0, 20), (4, 12), (2, 14), (3, 14), (1, 19), (1, 20), (0, 21), (2, 17), (5, 12), (3, 17), (2, 16),
    (3, 16), (3, 15), (1, 21), (0, 23), (2, 18), (0, 22), (4, 13), (4, 14), (2, 19), (2, 20), (3, 18), (1, 23),
    (1, 22), (5, 13), (5, 14), (3, 19), (3, 20), (4, 17), (2, 21), (4, 18), (4, 16), (5, 17), (4, 15), (5, 15),
    (0, 24), (5, 16), (3, 21), (5, 18), (2, 23), (2, 22), (4, 19), (4, 20), (3, 23), (3, 22), (5, 19), (5, 20),
    (4, 21), (1, 24), (2, 24), (5, 21), (4, 23), (4, 22), (5, 23), (5, 22), (3, 24), (4, 24), (5, 24), (0, 25),
    (1, 25), (2, 25), (3, 25), (4, 25), (5, 25),
)
MESH = pl.DeviceIdType.MESH

epsilon = 1e-05


def normalize(groups):
    power = jnp.mean(groups * groups, axis=-1, keepdims=True)
    return (groups * lax.rsqrt(power + epsilon)).astype(jnp.bfloat16)


def gelu(v):
    return 0.5 * v * (1.0 + lax.erf(v * (0.5**0.5)))


class Ring:
    def __init__(self, place, bit, forward, backward, mate):
        self.place, self.bit = place, bit
        self.forward, self.backward, self.mate = forward, backward, mate

    def slot(self, step, other):
        bit = 1 - self.bit if other else self.bit
        return lax.rem(self.place + step + 4, 4) * 2 + bit


def block_kernel(slot_ref, tiles_ref, block_ref, flipped_ref):
    place = pl.program_id(0)
    for col in range(block_ref.shape[1] // TILE):
        slot = slot_ref[place * (block_ref.shape[1] // TILE) + col]
        tile = tiles_ref[jnp.maximum(slot, 0)]
        tile = jnp.where(slot >= 0, tile, jnp.zeros_like(tile))
        block_ref[:, col * TILE : (col + 1) * TILE] = tile
        flipped_ref[col * TILE : (col + 1) * TILE, :] = tile.T


def build_block(slot_of, tile_values, row_tiles, col_tiles):
    rows, cols = row_tiles * TILE, col_tiles * TILE
    return pl.pallas_call(
        block_kernel,
        grid_spec=pltpu.PrefetchScalarGridSpec(
            num_scalar_prefetch=1,
            grid=(row_tiles,),
            in_specs=[pl.BlockSpec(tile_values.shape, lambda i, s: (0, 0, 0))],
            out_specs=[
                pl.BlockSpec((TILE, cols), lambda i, s: (i, 0)),
                pl.BlockSpec((cols, TILE), lambda i, s: (0, i)),
            ],
        ),
        out_shape=[
            jax.ShapeDtypeStruct((rows, cols), jnp.bfloat16),
            jax.ShapeDtypeStruct((cols, rows), jnp.bfloat16),
        ],
        cost_estimate=pl.CostEstimate(flops=0, bytes_accessed=24 << 20, transcendentals=0),
        name="build_block",
    )(slot_of, tile_values)


def hops_kernel(
    features_ref, block_hbm, flipped_hbm, mix_in_ref, mix_out_ref, out_ref,
    block, flipped, panel, back, hidden, ahead, across,
    row_near, row_pair, row_sum, row_mate, col_near, col_pair, col_sum, col_mate,
    local_sem, panel_send, panel_recv, core_send, core_recv, hidden_send, hidden_recv,
    row_send, row_recv, col_send, col_recv, swap_send, swap_recv,
):
    width = panel.shape[-1]
    r, q = lax.axis_index("row"), lax.axis_index("col")
    core, y, xl = lax.rem(q, 2), lax.rem(q // 2, 4), q // 8
    z, xh = r // 2, lax.rem(r, 2)

    def col_of(xl_, y_, core_):
        return {"col": (xl_ * 4 + y_) * 2 + core_}

    def row_of(z_, xh_):
        return {"row": z_ * 2 + xh_}

    partner = col_of(xl, y, 1 - core)
    col_ring = Ring(
        y, xl, col_of(xl, lax.rem(y + 1, 4), core), col_of(xl, lax.rem(y + 3, 4), core), col_of(1 - xl, y, core)
    )
    row_ring = Ring(
        z, xh, row_of(lax.rem(z + 1, 4), xh), row_of(lax.rem(z + 3, 4), xh), row_of(z, 1 - xh)
    )

    block_copy = pltpu.make_async_copy(block_hbm, block, local_sem.at[0])
    flipped_copy = pltpu.make_async_copy(flipped_hbm, flipped, local_sem.at[1])
    flipped_copy.start()
    block_copy.start()

    barrier = pltpu.get_barrier_semaphore()
    neighbours = [partner] + [d for g in (col_ring, row_ring) for d in (g.forward, g.backward, g.mate)]
    for device in neighbours:
        pl.semaphore_signal(barrier, inc=1, device_id=device, device_id_type=MESH)
    pl.semaphore_wait(barrier, len(neighbours))

    sent = []

    def send(src, dst, send_sem, recv_sem, device):
        copy = pltpu.make_async_remote_copy(
            src_ref=src, dst_ref=dst, send_sem=send_sem, recv_sem=recv_sem, device_id=device, device_id_type=MESH
        )
        copy.start()
        sent.append(copy)

    def await_recv(dst, send_sem, recv_sem, device):
        pltpu.make_async_remote_copy(
            src_ref=dst, dst_ref=dst, send_sem=send_sem, recv_sem=recv_sem, device_id=device, device_id_type=MESH
        ).wait_recv()

    class Gather:
        def __init__(self, c, ring, buf, base, send_sem, recv_sem):
            self.c, self.ring, self.buf, self.base = c, ring, buf, base
            self.ss, self.rs = send_sem, recv_sem
            self.slots = [
                ring.slot(0, True), ring.slot(-1, False), ring.slot(1, False), ring.slot(-1, True),
                ring.slot(1, True), ring.slot(2, False), ring.slot(2, True),
            ]

        def at(self, slot):
            return self.buf.at[self.c, self.base + slot]

        def push(self, src, slot, kind, device):
            send(src, self.at(slot), self.ss.at[self.c, kind], self.rs.at[self.c, kind], device)

        def wait(self, kind):
            await_recv(self.at(self.slots[kind]), self.ss.at[self.c, kind], self.rs.at[self.c, kind], self.ring.mate)

        def first(self, src):
            own = self.ring.slot(0, False)
            self.push(src, own, 0, self.ring.mate)
            self.push(src, own, 1, self.ring.forward)
            self.push(src, own, 2, self.ring.backward)

        def second(self):
            self.wait(0)
            slot = self.slots[0]
            self.push(self.at(slot), slot, 3, self.ring.forward)
            self.push(self.at(slot), slot, 4, self.ring.backward)

        def relay(self, kind):
            self.wait(kind)
            slot = self.slots[kind]
            if kind == 1:
                self.push(self.at(slot), slot, 5, self.ring.forward)
            if kind == 4:
                self.push(self.at(slot), slot, 6, self.ring.backward)

    class Scatter:
        def __init__(self, c, ring, buf, base, near, pair, total, mate, send_sem, recv_sem):
            self.c, self.ring, self.buf, self.base = c, ring, buf, base
            self.near, self.pair, self.total, self.mate = near, pair, total, mate
            self.ss, self.rs = send_sem, recv_sem

        def at(self, slot):
            return self.buf.at[self.c, self.base + slot]

        def group(self, step):
            return self.buf.at[self.c, pl.ds(self.base + lax.rem(self.ring.place + step + 4, 4) * 2, 2)]

        def push(self, src, dst, kind, device):
            send(src, dst, self.ss.at[self.c, kind], self.rs.at[self.c, kind], device)

        def wait(self, dst, kind):
            await_recv(dst, self.ss.at[self.c, kind], self.rs.at[self.c, kind], self.ring.mate)

        def first(self):
            self.push(self.at(self.ring.slot(2, False)), self.near.at[self.c, 0], 0, self.ring.forward)
            self.push(self.at(self.ring.slot(2, True)), self.near.at[self.c, 1], 1, self.ring.backward)

        def second(self, kind):
            step, other, device = ((1, False, self.ring.forward), (-1, True, self.ring.backward))[kind]
            self.wait(self.near.at[self.c, kind], kind)
            slot = self.base + self.ring.slot(step, other)
            self.buf[self.c, slot] = (
                self.buf[self.c, slot].astype(jnp.float32) + self.near[self.c, kind].astype(jnp.float32)
            ).astype(jnp.bfloat16)
            self.push(self.group(step), self.pair.at[self.c, kind], 2 + kind, device)

        def three(self, bit):
            slot = self.base + self.ring.place * 2 + bit
            return (
                self.buf[self.c, slot].astype(jnp.float32)
                + self.pair[self.c, 0, bit].astype(jnp.float32)
                + self.pair[self.c, 1, bit].astype(jnp.float32)
            )

        def third(self):
            self.wait(self.pair.at[self.c, 0], 2)
            self.wait(self.pair.at[self.c, 1], 3)
            self.total[self.c] = self.three(1 - self.ring.bit).astype(jnp.bfloat16)
            self.push(self.total.at[self.c], self.mate.at[self.c], 4, self.ring.mate)

        def last(self):
            self.wait(self.mate.at[self.c], 4)
            return self.three(self.ring.bit) + self.mate[self.c].astype(jnp.float32)

    class Chunk:
        def __init__(self, c):
            self.c = c
            self.cols = slice(c * width, (c + 1) * width)
            self.mine = core * 8
            self.spread = Gather(c, col_ring, panel, self.mine, panel_send, panel_recv)
            self.back = Scatter(
                c, row_ring, back, 0, row_near, row_pair, row_sum, row_mate, row_send, row_recv
            )
            self.share = Gather(c, row_ring, hidden, 0, hidden_send, hidden_recv)
            self.ahead = Scatter(
                c, col_ring, ahead, self.mine, col_near, col_pair, col_sum, col_mate, col_send, col_recv
            )

        def to_partner(self, src, slot, kind):
            send(
                src, panel.at[self.c, self.mine + slot],
                core_send.at[self.c, kind], core_recv.at[self.c, kind], partner,
            )

        def pass_on(self, kind):
            slot = self.spread.slots[kind]
            self.to_partner(self.spread.at(slot), slot, kind)

        def begin(self):
            own = features_ref.at[:, self.cols]
            self.spread.first(own)
            self.to_partner(own, col_ring.slot(0, False), 7)
            panel[self.c, self.mine + col_ring.slot(0, False)] = features_ref[:, self.cols]

        def spread_mate(self):
            self.spread.second()
            self.pass_on(0)

        def spread_relay(self, kind):
            self.spread.relay(kind)
            self.pass_on(kind)

        def back_product(self):
            theirs = (1 - core) * 8
            slots = self.spread.slots + [col_ring.slot(0, False)]
            for kind in range(8):
                await_recv(
                    panel.at[self.c, theirs + slots[kind]],
                    core_send.at[self.c, kind], core_recv.at[self.c, kind], partner,
                )
            if self.c == 0:
                flipped_copy.wait()

            @pl.loop(0, 2)
            def _(i):
                lhs = flipped[pl.ds(pl.multiple_of(i * 512, 512), 512), :]
                part = jnp.dot(
                    lhs, panel[self.c].reshape(16 * PIECE, width), preferred_element_type=jnp.float32
                )
                back[self.c, pl.ds(i * 4, 4)] = part.astype(jnp.bfloat16).reshape(4, PIECE, width)

            self.back.first()

        def encode(self):
            sums = self.back.last()
            own = row_ring.slot(0, False)
            for k in range(width // CH):
                mixed = jnp.dot(
                    normalize(sums[:, k * CH : (k + 1) * CH]), mix_in_ref[...], preferred_element_type=jnp.float32
                )
                hidden[self.c, own, :, k * CH : (k + 1) * CH] = gelu(mixed).astype(jnp.bfloat16)
            self.share.first(self.share.at(own))

        def ahead_product(self):
            if self.c == 0:
                block_copy.wait()

            @pl.loop(0, 4)
            def _(i):
                half = lax.rem(i // 2 + 1 - core + 2, 2)
                place = half * 2 + lax.rem(i, 2)
                lhs = block[pl.ds(pl.multiple_of(place * 512, 512), 512), :]
                part = jnp.dot(
                    lhs, hidden[self.c].reshape(8 * PIECE, width), preferred_element_type=jnp.float32
                )
                ahead[self.c, pl.ds(place * 4, 4)] = part.astype(jnp.bfloat16).reshape(4, PIECE, width)

            send(
                ahead.at[self.c, pl.ds((1 - core) * 8, 8)], across.at[self.c],
                swap_send.at[self.c], swap_recv.at[self.c], partner,
            )

        def join_cores(self):
            await_recv(across.at[self.c], swap_send.at[self.c], swap_recv.at[self.c], partner)

            @pl.loop(0, 8)
            def _(i):
                ahead[self.c, self.mine + i] = (
                    ahead[self.c, self.mine + i].astype(jnp.float32) + across[self.c, i].astype(jnp.float32)
                ).astype(jnp.bfloat16)

            self.ahead.first()

        def decode(self):
            sums = self.ahead.last()
            for k in range(width // CH):
                at = slice(self.c * width + k * CH, self.c * width + (k + 1) * CH)
                recon = jnp.dot(
                    normalize(sums[:, k * CH : (k + 1) * CH]), mix_out_ref[...], preferred_element_type=jnp.float32
                )
                out_ref[:, at] = recon

        def steps(self):
            part = functools.partial
            return [
                self.begin,
                self.spread_mate,
                *[part(self.spread_relay, kind) for kind in range(1, 7)],
                self.back_product,
                part(self.back.second, 0),
                part(self.back.second, 1),
                self.back.third,
                self.encode,
                self.share.second,
                *[part(self.share.relay, kind) for kind in range(1, 7)],
                self.ahead_product,
                self.join_cores,
                part(self.ahead.second, 0),
                part(self.ahead.second, 1),
                self.ahead.third,
                self.decode,
            ]

    steps = [Chunk(c).steps() for c in range(CHUNKS)]
    for c, step in ORDER:
        steps[c][step]()
    for copy in sent:
        copy.wait_send()


def two_hops(features, block, flipped, mix_in, mix_out):
    feat = features.shape[1]
    width = feat // CHUNKS
    dma = pltpu.SemaphoreType.DMA

    def buf(*shape):
        return pltpu.VMEM((CHUNKS,) + shape + (PIECE, width), jnp.bfloat16)

    vmem = pl.BlockSpec(memory_space=pltpu.VMEM)
    hbm = pl.BlockSpec(memory_space=pl.ANY)
    scatter = [buf(2), buf(2, 2), buf(), buf()]
    return pl.pallas_call(
        hops_kernel,
        out_shape=jax.ShapeDtypeStruct((PIECE, feat), jnp.float32),
        in_specs=[vmem, hbm, hbm, vmem, vmem],
        out_specs=vmem,
        scratch_shapes=[
            pltpu.VMEM(block.shape, jnp.bfloat16),
            pltpu.VMEM(flipped.shape, jnp.bfloat16),
            buf(16), buf(8), buf(8), buf(16), buf(8),
            *scatter, *scatter,
            dma((2,)),
            dma((CHUNKS, 7)), dma((CHUNKS, 7)),
            dma((CHUNKS, 8)), dma((CHUNKS, 8)),
            dma((CHUNKS, 7)), dma((CHUNKS, 7)),
            dma((CHUNKS, 5)), dma((CHUNKS, 5)),
            dma((CHUNKS, 5)), dma((CHUNKS, 5)),
            dma((CHUNKS,)), dma((CHUNKS,)),
        ],
        compiler_params=pltpu.CompilerParams(
            collective_id=0, has_side_effects=True, vmem_limit_bytes=60 << 20
        ),
        name="two_hops",
    )(features, block, flipped, mix_in, mix_out)


def local(ingest_features, node_map, unit_rows, tile_ids, tile_values, mix_in, mix_out):
    row_count = lax.axis_size("row")
    col_count = lax.axis_size("col")
    unit_count = row_count * col_count
    slots_held = node_map.shape[0]
    per_pair = slots_held // unit_count
    feature_width = ingest_features.shape[1]
    row_tiles = col_count * PIECE // TILE
    col_tiles = row_count * PIECE // TILE

    local_rows = tile_ids[:, 0] - lax.axis_index("row") * row_tiles
    local_cols = tile_ids[:, 1] - lax.axis_index("col") * col_tiles
    place = (lax.rem(local_rows, 2) * 4 + lax.rem(local_rows // 2, 4)) * 2 + local_rows // 8
    real = tile_ids[:, 0] < unit_count * PIECE // TILE
    spot = jnp.where(real, place * col_tiles + local_cols, -1)
    slot_ids = jnp.arange(tile_ids.shape[0], dtype=jnp.int32)
    slot_of = jnp.max(
        jnp.where(
            spot[None, :] == jnp.arange(row_tiles * col_tiles, dtype=jnp.int32)[:, None], slot_ids[None, :], -1
        ),
        axis=1,
    )
    block, flipped = build_block(slot_of, tile_values, row_tiles, col_tiles)

    owner = node_map // PIECE
    slot = jnp.arange(slots_held, dtype=jnp.int32)
    live = slot < unit_rows[0]
    same = (owner[:, None] == owner[None, :]) & live[None, :] & (slot[None, :] < slot[:, None])
    rank_within = jnp.sum(same.astype(jnp.int32), axis=1)
    target = jnp.where(live, owner * per_pair + rank_within, -1)
    pick = (target[None, :] == slot[:, None]).astype(jnp.bfloat16)
    marks = jnp.broadcast_to((node_map % PIECE + 1).astype(jnp.bfloat16)[:, None], (slots_held, CH))
    outgoing = jnp.dot(
        pick, jnp.concatenate([ingest_features, marks], axis=1), preferred_element_type=jnp.float32
    ).astype(jnp.bfloat16)
    arrived = lax.all_to_all(
        outgoing.reshape(unit_count, per_pair, feature_width + CH),
        ("row", "col"),
        split_axis=0,
        concat_axis=0,
        tiled=True,
    ).reshape(-1, feature_width + CH)
    arrived_at = arrived[:, feature_width].astype(jnp.int32) - 1
    put = (arrived_at[None, :] == jnp.arange(PIECE, dtype=jnp.int32)[:, None]).astype(jnp.bfloat16)
    features = jnp.dot(put, arrived[:, :feature_width], preferred_element_type=jnp.float32).astype(jnp.bfloat16)
    return features.astype(jnp.float32) - two_hops(features, block, flipped, mix_in, mix_out)


def solution(mesh):
    return jax.shard_map(
        local,
        mesh=mesh,
        in_specs=(
            P(("row", "col"), None),
            P(("row", "col")),
            P(("row", "col")),
            P(("row", "col"), None),
            P(("row", "col"), None, None),
            P(),
            P(),
        ),
        out_specs=P(("row", "col"), None),
        check_vma=False,
    )
```

```python
import functools

import jax
import jax.numpy as jnp
from jax import lax
from jax.experimental import pallas as pl
from jax.experimental.pallas import tpu as pltpu
from jax.sharding import PartitionSpec as P

CH = 128
TILE = 128
PIECE = 128
CHUNKS = 6
ORDER = (
    (0, 0), (1, 0), (2, 0), (0, 1), (0, 3), (0, 2), (1, 1), (1, 3), (1, 2), (2, 1), (2, 3), (2, 2), (0, 5), (0, 4),
    (0, 6), (1, 5), (3, 0), (2, 5), (1, 4), (0, 7), (1, 6), (3, 1), (1, 7), (0, 8), (3, 3), (2, 6), (1, 8), (2, 7),
    (3, 2), (2, 4), (3, 5), (0, 10), (0, 9), (2, 8), (1, 10), (3, 6), (1, 9), (3, 7), (3, 4), (4, 0), (5, 0),
    (3, 8), (4, 1), (4, 3), (2, 10), (4, 2), (2, 9), (5, 1), (5, 3), (5, 2), (0, 11), (4, 5), (4, 4), (1, 11),
    (3, 10), (4, 6), (5, 5), (3, 9), (0, 12), (4, 7), (5, 4), (5, 6), (1, 12), (5, 7), (4, 8), (0, 13), (0, 14),
    (0, 15), (1, 13), (1, 14), (1, 15), (5, 8), (4, 10), (4, 9), (0, 17), (0, 16), (2, 11), (0, 18), (1, 17),
    (3, 11), (5, 10), (1, 16), (1, 18), (2, 12), (5, 9), (3, 12), (0, 19), (0, 20), (2, 13), (1, 19), (1, 20),
    (3, 13), (2, 14), (0, 21), (2, 15), (4, 11), (5, 11), (1, 21), (3, 14), (3, 15), (0, 22), (0, 23), (2, 17),
    (2, 16), (3, 17), (4, 12), (1, 22), (1, 23), (2, 18), (3, 16), (5, 12), (2, 19), (2, 20), (3, 18), (4, 14),
    (4, 13), (3, 19), (3, 20), (5, 13), (5, 14), (0, 24), (2, 21), (4, 18), (4, 17), (1, 24), (4, 15), (5, 15),
    (4, 16), (3, 21), (5, 17), (2, 22), (2, 23), (4, 19), (4, 20), (5, 18), (3, 22), (3, 23), (5, 19), (5, 16),
    (5, 20), (4, 21), (2, 24), (5, 21), (3, 24), (4, 22), (4, 23), (5, 22), (5, 23), (4, 24), (5, 24), (0, 25),
    (1, 25), (2, 25), (3, 25), (4, 25), (5, 25),
)
MESH = pl.DeviceIdType.MESH

epsilon = 1e-05


def normalize(groups):
    power = jnp.mean(groups * groups, axis=-1, keepdims=True)
    return (groups * lax.rsqrt(power + epsilon)).astype(jnp.bfloat16)


def gelu(v):
    return 0.5 * v * (1.0 + lax.erf(v * (0.5**0.5)))


class Ring:
    def __init__(self, place, bit, forward, backward, mate):
        self.place, self.bit = place, bit
        self.forward, self.backward, self.mate = forward, backward, mate

    def slot(self, step, other):
        bit = 1 - self.bit if other else self.bit
        return lax.rem(self.place + step + 4, 4) * 2 + bit


def block_kernel(slot_ref, tiles_ref, block_ref, flipped_ref):
    place = pl.program_id(0)
    for col in range(block_ref.shape[1] // TILE):
        slot = slot_ref[place * (block_ref.shape[1] // TILE) + col]
        tile = tiles_ref[jnp.maximum(slot, 0)]
        tile = jnp.where(slot >= 0, tile, jnp.zeros_like(tile))
        block_ref[:, col * TILE : (col + 1) * TILE] = tile
        flipped_ref[col * TILE : (col + 1) * TILE, :] = tile.T


def build_block(slot_of, tile_values, row_tiles, col_tiles):
    rows, cols = row_tiles * TILE, col_tiles * TILE
    return pl.pallas_call(
        block_kernel,
        grid_spec=pltpu.PrefetchScalarGridSpec(
            num_scalar_prefetch=1,
            grid=(row_tiles,),
            in_specs=[pl.BlockSpec(tile_values.shape, lambda i, s: (0, 0, 0))],
            out_specs=[
                pl.BlockSpec((TILE, cols), lambda i, s: (i, 0)),
                pl.BlockSpec((cols, TILE), lambda i, s: (0, i)),
            ],
        ),
        out_shape=[
            jax.ShapeDtypeStruct((rows, cols), jnp.bfloat16),
            jax.ShapeDtypeStruct((cols, rows), jnp.bfloat16),
        ],
        cost_estimate=pl.CostEstimate(flops=0, bytes_accessed=24 << 20, transcendentals=0),
        name="build_block",
    )(slot_of, tile_values)


def hops_kernel(
    features_ref, block_hbm, flipped_hbm, mix_in_ref, mix_out_ref, out_ref,
    block, flipped, panel, back, hidden, ahead, across,
    row_near, row_pair, row_sum, row_mate, col_near, col_pair, col_sum, col_mate,
    local_sem, panel_send, panel_recv, core_send, core_recv, hidden_send, hidden_recv,
    row_send, row_recv, col_send, col_recv, swap_send, swap_recv,
):
    width = panel.shape[-1]
    r, q = lax.axis_index("row"), lax.axis_index("col")
    core, y, xl = lax.rem(q, 2), lax.rem(q // 2, 4), q // 8
    z, xh = r // 2, lax.rem(r, 2)

    def col_of(xl_, y_, core_):
        return {"col": (xl_ * 4 + y_) * 2 + core_}

    def row_of(z_, xh_):
        return {"row": z_ * 2 + xh_}

    partner = col_of(xl, y, 1 - core)
    col_ring = Ring(
        y, xl, col_of(xl, lax.rem(y + 1, 4), core), col_of(xl, lax.rem(y + 3, 4), core), col_of(1 - xl, y, core)
    )
    row_ring = Ring(
        z, xh, row_of(lax.rem(z + 1, 4), xh), row_of(lax.rem(z + 3, 4), xh), row_of(z, 1 - xh)
    )

    block_copy = pltpu.make_async_copy(block_hbm, block, local_sem.at[0])
    flipped_copy = pltpu.make_async_copy(flipped_hbm, flipped, local_sem.at[1])
    flipped_copy.start()
    block_copy.start()

    barrier = pltpu.get_barrier_semaphore()
    neighbours = [partner] + [d for g in (col_ring, row_ring) for d in (g.forward, g.backward, g.mate)]
    for device in neighbours:
        pl.semaphore_signal(barrier, inc=1, device_id=device, device_id_type=MESH)
    pl.semaphore_wait(barrier, len(neighbours))

    sent = []

    def send(src, dst, send_sem, recv_sem, device):
        copy = pltpu.make_async_remote_copy(
            src_ref=src, dst_ref=dst, send_sem=send_sem, recv_sem=recv_sem, device_id=device, device_id_type=MESH
        )
        copy.start()
        sent.append(copy)

    def await_recv(dst, send_sem, recv_sem, device):
        pltpu.make_async_remote_copy(
            src_ref=dst, dst_ref=dst, send_sem=send_sem, recv_sem=recv_sem, device_id=device, device_id_type=MESH
        ).wait_recv()

    class Gather:
        def __init__(self, c, ring, buf, base, send_sem, recv_sem):
            self.c, self.ring, self.buf, self.base = c, ring, buf, base
            self.ss, self.rs = send_sem, recv_sem
            self.slots = [
                ring.slot(0, True), ring.slot(-1, False), ring.slot(1, False), ring.slot(-1, True),
                ring.slot(1, True), ring.slot(2, False), ring.slot(2, True),
            ]

        def at(self, slot):
            return self.buf.at[self.c, self.base + slot]

        def push(self, src, slot, kind, device):
            send(src, self.at(slot), self.ss.at[self.c, kind], self.rs.at[self.c, kind], device)

        def wait(self, kind):
            await_recv(self.at(self.slots[kind]), self.ss.at[self.c, kind], self.rs.at[self.c, kind], self.ring.mate)

        def first(self, src):
            own = self.ring.slot(0, False)
            self.push(src, own, 0, self.ring.mate)
            self.push(src, own, 1, self.ring.forward)
            self.push(src, own, 2, self.ring.backward)

        def second(self):
            self.wait(0)
            slot = self.slots[0]
            self.push(self.at(slot), slot, 3, self.ring.forward)
            self.push(self.at(slot), slot, 4, self.ring.backward)

        def relay(self, kind):
            self.wait(kind)
            slot = self.slots[kind]
            if kind == 1:
                self.push(self.at(slot), slot, 5, self.ring.forward)
            if kind == 4:
                self.push(self.at(slot), slot, 6, self.ring.backward)

    class Scatter:
        def __init__(self, c, ring, buf, base, near, pair, total, mate, send_sem, recv_sem):
            self.c, self.ring, self.buf, self.base = c, ring, buf, base
            self.near, self.pair, self.total, self.mate = near, pair, total, mate
            self.ss, self.rs = send_sem, recv_sem

        def at(self, slot):
            return self.buf.at[self.c, self.base + slot]

        def group(self, step):
            return self.buf.at[self.c, pl.ds(self.base + lax.rem(self.ring.place + step + 4, 4) * 2, 2)]

        def push(self, src, dst, kind, device):
            send(src, dst, self.ss.at[self.c, kind], self.rs.at[self.c, kind], device)

        def wait(self, dst, kind):
            await_recv(dst, self.ss.at[self.c, kind], self.rs.at[self.c, kind], self.ring.mate)

        def first(self):
            self.push(self.at(self.ring.slot(2, False)), self.near.at[self.c, 0], 0, self.ring.forward)
            self.push(self.at(self.ring.slot(2, True)), self.near.at[self.c, 1], 1, self.ring.backward)

        def second(self, kind):
            step, other, device = ((1, False, self.ring.forward), (-1, True, self.ring.backward))[kind]
            self.wait(self.near.at[self.c, kind], kind)
            slot = self.base + self.ring.slot(step, other)
            self.buf[self.c, slot] = (
                self.buf[self.c, slot].astype(jnp.float32) + self.near[self.c, kind].astype(jnp.float32)
            ).astype(jnp.bfloat16)
            self.push(self.group(step), self.pair.at[self.c, kind], 2 + kind, device)

        def three(self, bit):
            slot = self.base + self.ring.place * 2 + bit
            return (
                self.buf[self.c, slot].astype(jnp.float32)
                + self.pair[self.c, 0, bit].astype(jnp.float32)
                + self.pair[self.c, 1, bit].astype(jnp.float32)
            )

        def third(self):
            self.wait(self.pair.at[self.c, 0], 2)
            self.wait(self.pair.at[self.c, 1], 3)
            self.total[self.c] = self.three(1 - self.ring.bit).astype(jnp.bfloat16)
            self.push(self.total.at[self.c], self.mate.at[self.c], 4, self.ring.mate)

        def last(self):
            self.wait(self.mate.at[self.c], 4)
            return self.three(self.ring.bit) + self.mate[self.c].astype(jnp.float32)

    class Chunk:
        def __init__(self, c):
            self.c = c
            self.cols = slice(c * width, (c + 1) * width)
            self.mine = core * 8
            self.spread = Gather(c, col_ring, panel, self.mine, panel_send, panel_recv)
            self.back = Scatter(
                c, row_ring, back, 0, row_near, row_pair, row_sum, row_mate, row_send, row_recv
            )
            self.share = Gather(c, row_ring, hidden, 0, hidden_send, hidden_recv)
            self.ahead = Scatter(
                c, col_ring, ahead, self.mine, col_near, col_pair, col_sum, col_mate, col_send, col_recv
            )

        def to_partner(self, src, slot, kind):
            send(
                src, panel.at[self.c, self.mine + slot],
                core_send.at[self.c, kind], core_recv.at[self.c, kind], partner,
            )

        def pass_on(self, kind):
            slot = self.spread.slots[kind]
            self.to_partner(self.spread.at(slot), slot, kind)

        def begin(self):
            own = features_ref.at[:, self.cols]
            self.spread.first(own)
            self.to_partner(own, col_ring.slot(0, False), 7)
            panel[self.c, self.mine + col_ring.slot(0, False)] = features_ref[:, self.cols]

        def spread_mate(self):
            self.spread.second()
            self.pass_on(0)

        def spread_relay(self, kind):
            self.spread.relay(kind)
            self.pass_on(kind)

        def back_product(self):
            theirs = (1 - core) * 8
            slots = self.spread.slots + [col_ring.slot(0, False)]
            for kind in range(8):
                await_recv(
                    panel.at[self.c, theirs + slots[kind]],
                    core_send.at[self.c, kind], core_recv.at[self.c, kind], partner,
                )
            if self.c == 0:
                flipped_copy.wait()

            @pl.loop(0, 2)
            def _(i):
                lhs = flipped[pl.ds(pl.multiple_of(i * 512, 512), 512), :]
                part = jnp.dot(
                    lhs, panel[self.c].reshape(16 * PIECE, width), preferred_element_type=jnp.float32
                )
                back[self.c, pl.ds(i * 4, 4)] = part.astype(jnp.bfloat16).reshape(4, PIECE, width)

            self.back.first()

        def encode(self):
            sums = self.back.last()
            own = row_ring.slot(0, False)
            for k in range(width // CH):
                mixed = jnp.dot(
                    normalize(sums[:, k * CH : (k + 1) * CH]), mix_in_ref[...], preferred_element_type=jnp.float32
                )
                hidden[self.c, own, :, k * CH : (k + 1) * CH] = gelu(mixed).astype(jnp.bfloat16)
            self.share.first(self.share.at(own))

        def ahead_product(self):
            if self.c == 0:
                block_copy.wait()

            @pl.loop(0, 4)
            def _(i):
                half = lax.rem(i // 2 + 1 - core + 2, 2)
                place = half * 2 + lax.rem(i, 2)
                lhs = block[pl.ds(pl.multiple_of(place * 512, 512), 512), :]
                part = jnp.dot(
                    lhs, hidden[self.c].reshape(8 * PIECE, width), preferred_element_type=jnp.float32
                )
                ahead[self.c, pl.ds(place * 4, 4)] = part.astype(jnp.bfloat16).reshape(4, PIECE, width)

            send(
                ahead.at[self.c, pl.ds((1 - core) * 8, 8)], across.at[self.c],
                swap_send.at[self.c], swap_recv.at[self.c], partner,
            )

        def join_cores(self):
            await_recv(across.at[self.c], swap_send.at[self.c], swap_recv.at[self.c], partner)

            @pl.loop(0, 8)
            def _(i):
                ahead[self.c, self.mine + i] = (
                    ahead[self.c, self.mine + i].astype(jnp.float32) + across[self.c, i].astype(jnp.float32)
                ).astype(jnp.bfloat16)

            self.ahead.first()

        def decode(self):
            sums = self.ahead.last()
            for k in range(width // CH):
                at = slice(self.c * width + k * CH, self.c * width + (k + 1) * CH)
                recon = jnp.dot(
                    normalize(sums[:, k * CH : (k + 1) * CH]), mix_out_ref[...], preferred_element_type=jnp.float32
                )
                out_ref[:, at] = recon

        def steps(self):
            part = functools.partial
            return [
                self.begin,
                self.spread_mate,
                *[part(self.spread_relay, kind) for kind in range(1, 7)],
                self.back_product,
                part(self.back.second, 0),
                part(self.back.second, 1),
                self.back.third,
                self.encode,
                self.share.second,
                *[part(self.share.relay, kind) for kind in range(1, 7)],
                self.ahead_product,
                self.join_cores,
                part(self.ahead.second, 0),
                part(self.ahead.second, 1),
                self.ahead.third,
                self.decode,
            ]

    steps = [Chunk(c).steps() for c in range(CHUNKS)]
    for c, step in ORDER:
        steps[c][step]()
    for copy in sent:
        copy.wait_send()


def two_hops(features, block, flipped, mix_in, mix_out):
    feat = features.shape[1]
    width = feat // CHUNKS
    dma = pltpu.SemaphoreType.DMA

    def buf(*shape):
        return pltpu.VMEM((CHUNKS,) + shape + (PIECE, width), jnp.bfloat16)

    vmem = pl.BlockSpec(memory_space=pltpu.VMEM)
    hbm = pl.BlockSpec(memory_space=pl.ANY)
    scatter = [buf(2), buf(2, 2), buf(), buf()]
    return pl.pallas_call(
        hops_kernel,
        out_shape=jax.ShapeDtypeStruct((PIECE, feat), jnp.float32),
        in_specs=[vmem, hbm, hbm, vmem, vmem],
        out_specs=vmem,
        scratch_shapes=[
            pltpu.VMEM(block.shape, jnp.bfloat16),
            pltpu.VMEM(flipped.shape, jnp.bfloat16),
            buf(16), buf(8), buf(8), buf(16), buf(8),
            *scatter, *scatter,
            dma((2,)),
            dma((CHUNKS, 7)), dma((CHUNKS, 7)),
            dma((CHUNKS, 8)), dma((CHUNKS, 8)),
            dma((CHUNKS, 7)), dma((CHUNKS, 7)),
            dma((CHUNKS, 5)), dma((CHUNKS, 5)),
            dma((CHUNKS, 5)), dma((CHUNKS, 5)),
            dma((CHUNKS,)), dma((CHUNKS,)),
        ],
        compiler_params=pltpu.CompilerParams(
            collective_id=0, has_side_effects=True, vmem_limit_bytes=60 << 20
        ),
        name="two_hops",
    )(features, block, flipped, mix_in, mix_out)


def local(ingest_features, node_map, unit_rows, tile_ids, tile_values, mix_in, mix_out):
    row_count = lax.axis_size("row")
    col_count = lax.axis_size("col")
    unit_count = row_count * col_count
    slots_held = node_map.shape[0]
    per_pair = slots_held // unit_count
    feature_width = ingest_features.shape[1]
    row_tiles = col_count * PIECE // TILE
    col_tiles = row_count * PIECE // TILE

    local_rows = tile_ids[:, 0] - lax.axis_index("row") * row_tiles
    local_cols = tile_ids[:, 1] - lax.axis_index("col") * col_tiles
    place = (lax.rem(local_rows, 2) * 4 + lax.rem(local_rows // 2, 4)) * 2 + local_rows // 8
    real = tile_ids[:, 0] < unit_count * PIECE // TILE
    spot = jnp.where(real, place * col_tiles + local_cols, -1)
    slot_ids = jnp.arange(tile_ids.shape[0], dtype=jnp.int32)
    slot_of = jnp.max(
        jnp.where(
            spot[None, :] == jnp.arange(row_tiles * col_tiles, dtype=jnp.int32)[:, None], slot_ids[None, :], -1
        ),
        axis=1,
    )
    block, flipped = build_block(slot_of, tile_values, row_tiles, col_tiles)

    owner = node_map // PIECE
    slot = jnp.arange(slots_held, dtype=jnp.int32)
    live = slot < unit_rows[0]
    same = (owner[:, None] == owner[None, :]) & live[None, :] & (slot[None, :] < slot[:, None])
    rank_within = jnp.sum(same.astype(jnp.int32), axis=1)
    target = jnp.where(live, owner * per_pair + rank_within, -1)
    pick = (target[None, :] == slot[:, None]).astype(jnp.bfloat16)
    marks = jnp.broadcast_to((node_map % PIECE + 1).astype(jnp.bfloat16)[:, None], (slots_held, CH))
    outgoing = jnp.dot(
        pick, jnp.concatenate([ingest_features, marks], axis=1), preferred_element_type=jnp.float32
    ).astype(jnp.bfloat16)
    arrived = lax.all_to_all(
        outgoing.reshape(unit_count, per_pair, feature_width + CH),
        ("row", "col"),
        split_axis=0,
        concat_axis=0,
        tiled=True,
    ).reshape(-1, feature_width + CH)
    arrived_at = arrived[:, feature_width].astype(jnp.int32) - 1
    put = (arrived_at[None, :] == jnp.arange(PIECE, dtype=jnp.int32)[:, None]).astype(jnp.bfloat16)
    features = jnp.dot(put, arrived[:, :feature_width], preferred_element_type=jnp.float32).astype(jnp.bfloat16)
    return features.astype(jnp.float32) - two_hops(features, block, flipped, mix_in, mix_out)


def solution(mesh):
    return jax.shard_map(
        local,
        mesh=mesh,
        in_specs=(
            P(("row", "col"), None),
            P(("row", "col")),
            P(("row", "col")),
            P(("row", "col"), None),
            P(("row", "col"), None, None),
            P(),
            P(),
        ),
        out_specs=P(("row", "col"), None),
        check_vma=False,
    )
```
